32 devices in a mesh: groups: 2 (over y), cand: 4 (over z), tgt: 2 (over x), mix: 2 (over core).
Axes of the slice: x: 2, y: 2, z: 4, core: 2. Of those that a mesh axis runs over, the one named last changes fastest.
Arguments:
- candidates: bfloat16 [8192, 1024], P(('groups', 'cand')), parts along dimension 0, may hold values from -6 to 6
- targets: bfloat16 [4096, 1024], P(('groups', 'tgt')), parts along dimension 0, may hold values from -6 to 6
- member: int32 [4096], P('groups'), parts along dimension 0, may hold values from 0 to 15
- mix_weight: float32 [64, 32], P('mix', 'groups'), parts along dimension 1, may hold values from 0.1 to 10
Outputs:
- cand_potential: float32 [64, 8192], P('mix', ('groups', 'cand')), parts along dimension 1
- tgt_potential: float32 [64, 4096], P('mix', ('groups', 'tgt')), parts along dimension 1
The draws below stay inside these ranges and needn't reach their ends.
There are 2 independent parts, one for each index of `groups`. The reference program is written for one: setup_inputs(seed, part) draws one part's arguments, and reference() takes and returns one part's arrays. A program takes and returns all parts, laid end to end along the dimension named above; each array names one. Nothing has to cross between parts.
All inputs are finite; a program needn't handle non-finite values.
Results may differ from the reference program's by a relative error of at most 0.0023.
Values sent between devices are 32-bit elements; how exact they have to be, the bound alone decides.
A program may use at most 64 MiB of HBM per device.

```python
import math
import jax
import jax.numpy as jnp
from jax import lax

E = 1024
MIX = 64
TASKS = 16
ITERS = 2
CD = 1024
NC = 4096
NT = 2048
N_CAND = 4


def cluster_axes(key):
    return jax.random.normal(jax.random.fold_in(key, 101), (TASKS, E), jnp.float32)


def member_ids(key):
    base_key = jax.random.fold_in(key, 102)
    first_key, second_key, third_key = jax.random.split(base_key, 3)
    task_ids = jax.random.randint(first_key, (NT,), 0, TASKS, dtype=jnp.int32)
    low_place = jax.random.randint(second_key, (), 0, NT, dtype=jnp.int32)
    high_step = jax.random.randint(third_key, (), 0, NT - 1, dtype=jnp.int32)
    high_place = (low_place + 1 + high_step) % NT
    places = jnp.arange(NT, dtype=jnp.int32)
    task_ids = jnp.where(places == low_place, 0, task_ids)
    task_ids = jnp.where(places == high_place, TASKS - 1, task_ids)
    return task_ids.astype(jnp.int32)


def draw_jitter(key, salt, rows):
    jitter_key = jax.random.fold_in(key, salt)
    return jax.random.normal(jitter_key, (rows, E), jnp.float32)


def draw_member(key, part):
    return member_ids(key)


def draw_targets(key, part):
    task_axes = cluster_axes(key)
    centre = jnp.take(task_axes, member_ids(key), axis=0)
    values = 0.5477226 * centre + 0.83666 * draw_jitter(key, 103, NT)
    return jnp.clip(values, -6.0, 6.0).astype(jnp.bfloat16)


def draw_candidates(key, part):
    task_axes = cluster_axes(key)
    pick_key = jax.random.fold_in(key, 104)
    gain_key = jax.random.fold_in(key, 105)
    task_picks = jax.random.randint(pick_key, (3, NC), 0, TASKS, dtype=jnp.int32)
    gain_rows = 0.35 * jnp.exp(0.5 * jax.random.normal(gain_key, (3, NC, 1), jnp.float32))
    values = 0.7071068 * draw_jitter(key, 106, NC)
    for picked in range(3):
        values = values + gain_rows[picked] * jnp.take(task_axes, task_picks[picked], axis=0)
    return jnp.clip(values, -6.0, 6.0).astype(jnp.bfloat16)


def shard_levels(key, dims, cuts, least, largest):
    loudness, own = 1.0, jax.random.fold_in(key, 6)
    for dim, parts in cuts:
        draws = jnp.exp(jax.random.uniform(jax.random.fold_in(own, dim), (parts,), jnp.float32, least / len(cuts), largest / len(cuts)))
        loudness = loudness * jnp.repeat(draws, dims[dim] // parts).reshape([-1 if axis == dim else 1 for axis in range(len(dims))])
    return loudness


def setup_inputs(seed: int = 0, part: int = 0) -> dict:
    streams_of = jax.random.split(jax.random.key(seed), 5)
    part_splits = jax.random.split(jax.random.fold_in(streams_of[4], part), 5)
    return {
        "candidates": draw_candidates(jax.random.fold_in(jax.random.fold_in(streams_of[4], part), 71), part),
        "targets": draw_targets(jax.random.fold_in(jax.random.fold_in(streams_of[4], part), 71), part),
        "member": draw_member(jax.random.fold_in(jax.random.fold_in(streams_of[4], part), 71), part),
        "mix_weight": jnp.clip(jnp.exp(math.log(10.0) - 4.6051702 * jax.random.uniform(part_splits[3], (MIX, TASKS), jnp.float32) ** shard_levels(part_splits[3], (MIX, TASKS), ((0, 2),), -0.2, 0.2)), 0.1, 10.0),
    }


EPS_FIRST = 0.05
EPS_SECOND = 0.025

def unit_rows(embedding):
    values = embedding.astype(jnp.float32)
    mean_sq = lax.optimization_barrier(jnp.mean(values * values, axis=1, keepdims=True))
    return (values * lax.rsqrt(mean_sq + 1e-06) * (1.0 / math.sqrt(values.shape[1]))).astype(jnp.bfloat16)

def contract_last(left, right):
    return lax.dot_general(left, right, (((1,), (1,)), ((), ())), preferred_element_type=jnp.float32)

def target_mass(own_member, member, mix_weight, cand_total):
    task_ids = jnp.arange(mix_weight.shape[1], dtype=jnp.int32)
    counts = lax.optimization_barrier(jnp.sum((member[None, :] == task_ids[:, None]).astype(jnp.float32), axis=1))
    weight_total = jnp.dot(mix_weight, counts, precision=lax.Precision.HIGHEST)
    onehot = (own_member[None, :] == task_ids[:, None]).astype(jnp.float32)
    per_target = jnp.dot(mix_weight, onehot, precision=lax.Precision.HIGHEST)
    return per_target * (cand_total / weight_total)[:, None]

def reference(candidates, targets, member, mix_weight):
    tgt_unit = unit_rows(targets)
    cand_blocks = unit_rows(candidates).reshape(N_CAND, CD, E)

    def score_block(cand_block):
        return contract_last(cand_block, tgt_unit)
    scores = lax.map(score_block, cand_blocks)
    mass = target_mass(member, member, mix_weight, float(NC))
    scale_tgt = jnp.ones((MIX, NT), jnp.float32)
    scale_blocks = jnp.zeros((N_CAND, MIX, CD), jnp.float32)
    for section_index, epsilon in enumerate((EPS_FIRST, EPS_SECOND)):
        if section_index == 1:
            scale_tgt = scale_tgt * scale_tgt
        for repeat in range(ITERS):

            def cand_pass(score_rows):
                kernel = jnp.exp(score_rows / epsilon) / NT
                return 1.0 / lax.dot_general(scale_tgt, kernel, (((1,), (1,)), ((), ())), precision=lax.Precision.HIGHEST)
            scale_blocks = lax.map(cand_pass, scores)

            def tgt_pass(column_sum, paired):
                kernel = jnp.exp(paired[0] / epsilon) / NT
                return (column_sum + jnp.dot(paired[1], kernel, precision=lax.Precision.HIGHEST), None)
            column_sum, unused = lax.scan(tgt_pass, jnp.zeros((MIX, NT), jnp.float32), (scores, scale_blocks))
            scale_tgt = mass / column_sum
    scale_cand = jnp.transpose(scale_blocks, (1, 0, 2)).reshape(MIX, NC)
    return (jnp.log(scale_cand), jnp.log(scale_tgt))
```

```python
import functools
import math

import jax
import jax.numpy as jnp
from jax import lax
from jax.experimental import pallas as pl
from jax.experimental.pallas import tpu as pltpu
from jax.sharding import PartitionSpec as P

ITERS = 2


EPS_FIRST = 0.05
EPS_SECOND = 0.025

MESH = pl.DeviceIdType.MESH
F32 = jnp.float32
BF16 = jnp.bfloat16
NT_DIMS = (((1,), (1,)), ((), ()))
NN_DIMS = (((1,), (0,)), ((), ()))


def unit_rows(embedding):
    values = embedding.astype(jnp.float32)
    mean_sq = jnp.mean(values * values, axis=1, keepdims=True)
    return (values * lax.rsqrt(mean_sq + 1e-06) * (1.0 / math.sqrt(values.shape[1]))).astype(
        jnp.bfloat16
    )


def contract_last(left, right):
    return lax.dot_general(left, right, NT_DIMS, preferred_element_type=jnp.float32)


def split_rows(value):
    head = value.astype(BF16)
    rest = (value - head.astype(F32)).astype(BF16)
    return jnp.concatenate([head, rest], axis=0)


def join_rows(value):
    half = value.shape[0] // 2
    return value[:half] + value[half:]


def fused_kernel(
    n_tgt, n_cand, cand_ref, tgt_ref, member_ref, weight_ref, out_cand, out_tgt,
    tgt_unit, k_one, k_two, mass, acc,
    row_slots, col_slots, task_slots, cand_slots, rs_send, rs_slots, ag_slots,
    x_send, x_recv, z_send, z_recv,
):
    xi, zi = lax.axis_index("tgt"), lax.axis_index("cand")
    rows, width = cand_ref.shape
    cols = tgt_ref.shape[0]
    mixes, tasks = weight_ref.shape
    share = cols // n_cand
    tgt_total, cand_total = cols * n_tgt, rows * n_cand

    def x_peer(d):
        return {"tgt": lax.rem(xi + d, n_tgt)}

    def z_peer(d):
        return {"cand": lax.rem(zi + d, n_cand)}

    barrier = pltpu.get_barrier_semaphore()
    for d in range(1, n_tgt):
        pl.semaphore_signal(barrier, inc=1, device_id=x_peer(d), device_id_type=MESH)
    for d in range(1, n_cand):
        pl.semaphore_signal(barrier, inc=1, device_id=z_peer(d), device_id_type=MESH)

    def send(src, dst, sems, phase, d, peer):
        copy = pltpu.make_async_remote_copy(
            src_ref=src, dst_ref=dst,
            send_sem=sems[0].at[phase, d - 1], recv_sem=sems[1].at[phase, d - 1],
            device_id=peer, device_id_type=MESH,
        )
        copy.start()
        pending.append(copy)
        return copy

    pending = []
    xs, zs = (x_send, x_recv), (z_send, z_recv)

    def x_sum(slots):
        total = slots[lax.rem(xi + n_tgt, n_tgt)]
        for k in range(1, n_tgt):
            total = total + slots[lax.rem(xi - k + n_tgt, n_tgt)]
        return total

    def z_sum(slots):
        total = slots[lax.rem(zi + n_cand, n_cand)]
        for k in range(1, n_cand):
            total = total + slots[lax.rem(zi - k + n_cand, n_cand)]
        return total

    def x_exchange(slots, phase):
        copies = [send(slots.at[0], slots.at[d], xs, phase, d, x_peer(d)) for d in range(1, n_tgt)]
        for copy in copies:
            copy.wait_recv()
        return x_sum(slots)

    block = 256

    def norm_targets(b, carry):
        at = pl.ds(pl.multiple_of(b * block, block), block)
        tgt_unit[at, :] = unit_rows(tgt_ref[at, :])
        return carry

    lax.fori_loop(0, cols // block, norm_targets, 0)

    def build(b, carry):
        at = pl.ds(pl.multiple_of(b * block, block), block)
        scores = contract_last(unit_rows(cand_ref[at, :]), tgt_unit[...])
        raised = jnp.exp(scores * (1.0 / EPS_FIRST))
        k_one[at, :] = (raised * (1.0 / tgt_total)).astype(BF16)
        k_two[at, :] = (raised * raised * (1.0 / tgt_total)).astype(BF16)
        return carry

    lax.fori_loop(0, rows // block, build, 0)

    all_ids = lax.broadcasted_iota(jnp.int32, (tasks, tgt_total), 0)
    all_hot = (member_ref[...] == all_ids).astype(F32)
    weights = weight_ref[...]
    per_target = lax.dot_general(
        weights, all_hot, NN_DIMS, precision=lax.Precision.HIGHEST, preferred_element_type=F32
    )
    ratio = float(cand_total) / jnp.sum(per_target, axis=1, keepdims=True)
    own = pl.ds(pl.multiple_of(xi * cols, cols), cols)
    own_hot = (
        member_ref[:, own] == lax.broadcasted_iota(jnp.int32, (tasks, cols), 0)
    ).astype(F32)
    mass[...] = (
        lax.dot_general(
            weights, own_hot, NN_DIMS, precision=lax.Precision.HIGHEST, preferred_element_type=F32
        )
        * ratio
    )

    pl.semaphore_wait(barrier, n_tgt - 1 + n_cand - 1)

    ones = jnp.ones((16, cols), BF16)
    row_slots[0] = contract_last(ones, k_one[...])[:1]
    scale_row = 1.0 / x_exchange(row_slots, 0)
    place = lax.broadcasted_iota(jnp.int32, (16, rows), 0)
    head = scale_row.astype(BF16).astype(F32)
    lhs = jnp.where(place == 0, head, jnp.where(place == 1, scale_row - head, 0.0)).astype(BF16)
    part = lax.dot_general(lhs, k_one[...], NN_DIMS, preferred_element_type=F32)
    col_slots[0] = part[:1] + part[1:2]
    copies = [
        send(col_slots.at[0], col_slots.at[d], zs, 0, d, z_peer(d)) for d in range(1, n_cand)
    ]
    for copy in copies:
        copy.wait_recv()
    col_sum = z_sum(col_slots)

    task_slots[0] = join_rows(contract_last(split_rows(own_hot / col_sum), k_one[...]))
    by_task = x_exchange(task_slots, 1)
    cand_sum = ratio * lax.dot_general(
        weights, by_task, NN_DIMS, precision=lax.Precision.HIGHEST, preferred_element_type=F32
    )

    def tgt_pass(cand_sum, kernel, turn):
        lhs = split_rows(1.0 / cand_sum)

        def columns(peer):
            at = pl.ds(pl.multiple_of(peer * share, share), share)
            return join_rows(
                lax.dot_general(lhs, kernel[:, at], NN_DIMS, preferred_element_type=F32)
            )

        copies = []
        for d in range(1, n_cand):
            rs_send[turn, d - 1] = columns(lax.rem(zi + d, n_cand))
            copies.append(
                send(rs_send.at[turn, d - 1], rs_slots.at[turn, d], zs, 1 + 2 * turn, d, z_peer(d))
            )
        rs_slots[turn, 0] = columns(zi)
        for copy in copies:
            copy.wait_recv()
        total = z_sum(rs_slots.at[turn])
        at = pl.ds(pl.multiple_of(zi * share, share), share)
        return mass[:, at] / total

    def gather(value, turn):
        ag_slots[turn, 0] = value
        return [
            send(ag_slots.at[turn, 0], ag_slots.at[turn, d], zs, 2 + 2 * turn, d, z_peer(d))
            for d in range(1, n_cand)
        ]

    def cand_pass(copies, turn):
        for d in range(n_cand):
            if d:
                copies[d - 1].wait_recv()
            at = pl.ds(pl.multiple_of(lax.rem(zi - d + n_cand, n_cand) * share, share), share)
            part = contract_last(split_rows(ag_slots[turn, d]), k_two[:, at])
            if d:
                acc[...] += part
            else:
                acc[...] = part
        cand_slots[turn, 0] = join_rows(acc[...])
        return x_exchange(cand_slots.at[turn], 2 + turn)

    scale = tgt_pass(cand_sum, k_one, 0)
    scale = scale * scale
    for repeat in range(ITERS):
        cand_sum = cand_pass(gather(scale, repeat), repeat)
        scale = tgt_pass(cand_sum, k_two, 1 + repeat)
    copies = gather(jnp.log(scale), ITERS)
    out_cand[...] = -jnp.log(cand_sum)
    for d in range(n_cand):
        if d:
            copies[d - 1].wait_recv()
        at = pl.ds(pl.multiple_of(lax.rem(zi - d + n_cand, n_cand) * share, share), share)
        out_tgt[:, at] = ag_slots[ITERS, d]
    for copy in pending:
        copy.wait_send()


def fused(candidates, targets, member, mix_weight):
    n_tgt, n_cand = lax.axis_size("tgt"), lax.axis_size("cand")
    rows, width = candidates.shape
    cols = targets.shape[0]
    mixes, tasks = mix_weight.shape
    share = cols // n_cand
    return tuple(pl.pallas_call(
        functools.partial(fused_kernel, n_tgt, n_cand),
        out_shape=(
            jax.ShapeDtypeStruct((mixes, rows), F32),
            jax.ShapeDtypeStruct((mixes, cols), F32),
        ),
        in_specs=[pl.BlockSpec(memory_space=pltpu.VMEM)] * 4,
        out_specs=(pl.BlockSpec(memory_space=pltpu.VMEM),) * 2,
        scratch_shapes=[
            pltpu.VMEM((cols, width), BF16),
            pltpu.VMEM((rows, cols), BF16),
            pltpu.VMEM((rows, cols), BF16),
            pltpu.VMEM((mixes, cols), F32),
            pltpu.VMEM((2 * mixes, rows), F32),
            pltpu.VMEM((n_tgt, 1, rows), F32),
            pltpu.VMEM((n_cand, 1, cols), F32),
            pltpu.VMEM((n_tgt, tasks, rows), F32),
            pltpu.VMEM((ITERS, n_tgt, mixes, rows), F32),
            pltpu.VMEM((1 + ITERS, n_cand - 1, mixes, share), F32),
            pltpu.VMEM((1 + ITERS, n_cand, mixes, share), F32),
            pltpu.VMEM((1 + ITERS, n_cand, mixes, share), F32),
            pltpu.SemaphoreType.DMA((2 + ITERS, n_tgt - 1)),
            pltpu.SemaphoreType.DMA((2 + ITERS, n_tgt - 1)),
            pltpu.SemaphoreType.DMA((3 + 2 * ITERS, n_cand - 1)),
            pltpu.SemaphoreType.DMA((3 + 2 * ITERS, n_cand - 1)),
        ],
        compiler_params=pltpu.CompilerParams(
            collective_id=0, has_side_effects=True, vmem_limit_bytes=48 * 1024 * 1024
        ),
    )(candidates, targets, member.reshape(1, -1), mix_weight))


def target_mass(own_member, member, mix_weight, cand_total):
    task_ids = jnp.arange(mix_weight.shape[1], dtype=jnp.int32)
    counts = jnp.sum((member[None, :] == task_ids[:, None]).astype(jnp.float32), axis=1)
    weight_total = jnp.dot(mix_weight, counts, precision=lax.Precision.HIGHEST)
    onehot = (own_member[None, :] == task_ids[:, None]).astype(jnp.float32)
    per_target = jnp.dot(mix_weight, onehot, precision=lax.Precision.HIGHEST)
    return per_target * (cand_total / weight_total)[:, None]


def by_collectives(candidates, targets, member, mix_weight):
    cand_rows = candidates.shape[0]
    tgt_rows = targets.shape[0]
    tgt_total = tgt_rows * lax.axis_size("tgt")
    cand_total = cand_rows * lax.axis_size("cand")
    tgt_unit = unit_rows(targets)
    scores = contract_last(unit_rows(candidates), tgt_unit)
    own_member = lax.dynamic_slice_in_dim(member, lax.axis_index("tgt") * tgt_rows, tgt_rows, 0)
    mass = target_mass(own_member, member, mix_weight, float(cand_total))
    kernel_one = jnp.exp(scores / EPS_FIRST) / tgt_total
    kernel_two = jnp.exp(scores / EPS_SECOND) / tgt_total
    scale_tgt = jnp.ones((mix_weight.shape[0], tgt_rows), jnp.float32)
    scale_cand = jnp.ones((mix_weight.shape[0], cand_rows), jnp.float32)
    for section_index, kernel in enumerate((kernel_one, kernel_two)):
        if section_index == 1:
            scale_tgt = scale_tgt * scale_tgt
        for repeat in range(ITERS):
            partial_value = lax.dot_general(
                scale_tgt, kernel, (((1,), (1,)), ((), ())), precision=lax.Precision.HIGHEST
            )
            scale_cand = 1.0 / lax.psum(partial_value, "tgt")
            column_part = jnp.dot(scale_cand, kernel, precision=lax.Precision.HIGHEST)
            share_cols = tgt_rows // lax.axis_size("cand")
            summed = lax.psum_scatter(column_part, "cand", scatter_dimension=1, tiled=True)
            own_mass = lax.dynamic_slice_in_dim(
                mass, lax.axis_index("cand") * share_cols, share_cols, 1
            )
            scale_tgt = lax.all_gather(own_mass / summed, "cand", axis=1, tiled=True)
    return (jnp.log(scale_cand), jnp.log(scale_tgt))


def solution(mesh):
    in_specs = (
        P(("groups", "cand"), None),
        P(("groups", "tgt"), None),
        P("groups"),
        P("mix", "groups"),
    )
    out_specs = (P("mix", ("groups", "cand")), P("mix", ("groups", "tgt")))
    n_tgt, n_cand = mesh.shape["tgt"], mesh.shape["cand"]

    def local(candidates, targets, member, mix_weight):
        lanes = targets.shape[0] % (128 * n_cand) == 0
        step = fused if lanes and n_cand > 1 and n_tgt > 1 else by_collectives
        return step(candidates, targets, member, mix_weight)

    return jax.shard_map(local, mesh=mesh, in_specs=in_specs, out_specs=out_specs, check_vma=False)
```

```python
import functools
import math

import jax
import jax.numpy as jnp
from jax import lax
from jax.experimental import pallas as pl
from jax.experimental.pallas import tpu as pltpu
from jax.sharding import PartitionSpec as P

ITERS = 2


EPS_FIRST = 0.05
EPS_SECOND = 0.025

MESH = pl.DeviceIdType.MESH
F32 = jnp.float32
BF16 = jnp.bfloat16
NT_DIMS = (((1,), (1,)), ((), ()))
NN_DIMS = (((1,), (0,)), ((), ()))


def unit_rows(embedding):
    values = embedding.astype(jnp.float32)
    mean_sq = jnp.mean(values * values, axis=1, keepdims=True)
    return (values * lax.rsqrt(mean_sq + 1e-06) * (1.0 / math.sqrt(values.shape[1]))).astype(
        jnp.bfloat16
    )


def contract_last(left, right):
    return lax.dot_general(left, right, NT_DIMS, preferred_element_type=jnp.float32)


def split_rows(value):
    head = value.astype(BF16)
    rest = (value - head.astype(F32)).astype(BF16)
    return jnp.concatenate([head, rest], axis=0)


def join_rows(value):
    half = value.shape[0] // 2
    return value[:half] + value[half:]


def fused_kernel(
    n_tgt, n_cand, parts, cand_hbm, tgt_hbm, member_ref, weight_ref, out_cand, out_tgt,
    cand_rows, tgt_rows, tgt_unit, raised, k_one, k_two, mass, cand_sums,
    row_slots, col_slots, task_slots, cand_slots, rs_send, rs_slots, ag_slots,
    load_sems, x_send, x_recv, z_send, z_recv,
):
    xi, zi = lax.axis_index("tgt"), lax.axis_index("cand")
    rows, width = cand_hbm.shape
    cols = tgt_hbm.shape[0]
    mixes, tasks = weight_ref.shape
    share = cols // n_cand
    group = mixes // parts
    tgt_total, cand_total = cols * n_tgt, rows * n_cand
    block = 256

    def loads(src, dst, row):
        return [
            pltpu.make_async_copy(
                src.at[pl.ds(at, block)], dst.at[pl.ds(at, block)], load_sems.at[row, at // block]
            )
            for at in range(0, src.shape[0], block)
        ]

    tgt_loads, cand_loads = loads(tgt_hbm, tgt_rows, 0), loads(cand_hbm, cand_rows, 1)
    for copy in tgt_loads + cand_loads:
        copy.start()

    def x_peer(d):
        return {"tgt": lax.rem(xi + d, n_tgt)}

    def z_peer(d):
        return {"cand": lax.rem(zi + d, n_cand)}

    barrier = pltpu.get_barrier_semaphore()
    for d in range(1, n_tgt):
        pl.semaphore_signal(barrier, inc=1, device_id=x_peer(d), device_id_type=MESH)
    for d in range(1, n_cand):
        pl.semaphore_signal(barrier, inc=1, device_id=z_peer(d), device_id_type=MESH)

    pending = []
    xs, zs = (x_send, x_recv), (z_send, z_recv)

    def send(src, dst, sems, phase, d, peer):
        copy = pltpu.make_async_remote_copy(
            src_ref=src, dst_ref=dst,
            send_sem=sems[0].at[phase, d - 1], recv_sem=sems[1].at[phase, d - 1],
            device_id=peer, device_id_type=MESH,
        )
        copy.start()
        pending.append(copy)
        return copy

    def x_sum(slots):
        total = slots[lax.rem(xi + n_tgt, n_tgt)]
        for k in range(1, n_tgt):
            total = total + slots[lax.rem(xi - k + n_tgt, n_tgt)]
        return total

    def z_sum(slots):
        total = slots[lax.rem(zi + n_cand, n_cand)]
        for k in range(1, n_cand):
            total = total + slots[lax.rem(zi - k + n_cand, n_cand)]
        return total

    def x_start(slots, phase):
        return [send(slots.at[0], slots.at[d], xs, phase, d, x_peer(d)) for d in range(1, n_tgt)]

    def z_start(slots, phase):
        return [send(slots.at[0], slots.at[d], zs, phase, d, z_peer(d)) for d in range(1, n_cand)]

    def arrive(copies):
        for copy in copies:
            copy.wait_recv()

    def z_columns(d):
        at = lax.rem(zi - d + n_cand, n_cand) * share
        return pl.ds(pl.multiple_of(at, share), share)

    all_ids = lax.broadcasted_iota(jnp.int32, (tasks, tgt_total), 0)
    all_hot = (member_ref[...] == all_ids).astype(F32)
    weights = weight_ref[...]
    per_target = lax.dot_general(
        weights, all_hot, NN_DIMS, precision=lax.Precision.HIGHEST, preferred_element_type=F32
    )
    ratio = float(cand_total) / jnp.sum(per_target, axis=1, keepdims=True)
    own = pl.ds(pl.multiple_of(xi * cols, cols), cols)
    own_hot = (
        member_ref[:, own] == lax.broadcasted_iota(jnp.int32, (tasks, cols), 0)
    ).astype(F32)
    mass[...] = (
        lax.dot_general(
            weights, own_hot, NN_DIMS, precision=lax.Precision.HIGHEST, preferred_element_type=F32
        )
        * ratio
    )

    for index, copy in enumerate(tgt_loads):
        copy.wait()
        at = pl.ds(index * block, block)
        tgt_unit[at, :] = unit_rows(tgt_rows[at, :])
    for index, copy in enumerate(cand_loads):
        copy.wait()
        at = pl.ds(index * block, block)
        scores = contract_last(unit_rows(cand_rows[at, :]), tgt_unit[...])
        power = jnp.exp(scores * (1.0 / EPS_FIRST))
        raised[at, :] = power
        k_one[at, :] = (power * (1.0 / tgt_total)).astype(BF16)

    def square(first, last):
        def step(b, carry):
            at = pl.ds(pl.multiple_of(b * 64, 64), 64)
            power = raised[at, :]
            k_two[at, :] = (power * power * (1.0 / tgt_total)).astype(BF16)
            return carry

        lax.fori_loop(first // 64, last // 64, step, 0)

    pl.semaphore_wait(barrier, n_tgt - 1 + n_cand - 1)

    ones = jnp.ones((16, cols), BF16)
    row_slots[0] = contract_last(ones, k_one[...])[:1]
    copies = x_start(row_slots, 0)
    square(0, rows // 2)
    arrive(copies)
    scale_row = 1.0 / x_sum(row_slots)
    place = lax.broadcasted_iota(jnp.int32, (16, rows), 0)
    head = scale_row.astype(BF16).astype(F32)
    lhs = jnp.where(place == 0, head, jnp.where(place == 1, scale_row - head, 0.0)).astype(BF16)
    part = lax.dot_general(lhs, k_one[...], NN_DIMS, preferred_element_type=F32)
    col_slots[0] = part[:1] + part[1:2]
    copies = z_start(col_slots, 0)
    square(rows // 2, rows)
    arrive(copies)
    col_sum = z_sum(col_slots)

    task_slots[0] = join_rows(contract_last(split_rows(own_hot / col_sum), k_one[...]))
    arrive(x_start(task_slots, 1))
    cand_sums[...] = ratio * lax.dot_general(
        weights, x_sum(task_slots), NN_DIMS, precision=lax.Precision.HIGHEST,
        preferred_element_type=F32,
    )

    def of(part):
        return pl.ds(part * group, group)

    def tgt_send(kernel, turn, part):
        lhs = split_rows(1.0 / cand_sums[of(part), :])

        def columns(peer):
            at = pl.ds(pl.multiple_of(peer * share, share), share)
            return join_rows(
                lax.dot_general(lhs, kernel[:, at], NN_DIMS, preferred_element_type=F32)
            )

        out, slots = rs_send.at[turn, part], rs_slots.at[turn, part]
        copies = []
        for d in range(1, n_cand):
            out[d - 1] = columns(lax.rem(zi + d, n_cand))
            copies.append(
                send(out.at[d - 1], slots.at[d], zs, 1 + turn * parts + part, d, z_peer(d))
            )
        slots[0] = columns(zi)
        return copies

    def tgt_finish(copies, turn, part, change):
        arrive(copies)
        slots = ag_slots.at[turn, part]
        slots[0] = change(mass[of(part), z_columns(0)] / z_sum(rs_slots.at[turn, part]))
        return z_start(slots, 1 + (1 + ITERS + turn) * parts + part)

    def cand_send(copies, turn, part):
        total = None
        for d in range(n_cand):
            if d:
                copies[d - 1].wait_recv()
            value = contract_last(split_rows(ag_slots[turn, part, d]), k_two[:, z_columns(d)])
            total = value if total is None else total + value
        cand_slots[turn, part, 0] = join_rows(total)
        return x_start(cand_slots.at[turn, part], 2 + turn * parts + part)

    def cand_finish(copies, turn, part):
        arrive(copies)
        cand_sums[of(part), :] = x_sum(cand_slots.at[turn, part])

    def keep(scale):
        return scale

    each = range(parts)
    reduced = [tgt_send(k_one, 0, part) for part in each]
    changes = (jnp.square,) + (keep,) * (ITERS - 1)
    for turn in range(ITERS):
        gathered = [tgt_finish(reduced[part], turn, part, changes[turn]) for part in each]
        summed = [cand_send(gathered[part], turn, part) for part in each]
        reduced = []
        for part in each:
            cand_finish(summed[part], turn, part)
            reduced.append(tgt_send(k_two, 1 + turn, part))
    out_cand[...] = -jnp.log(cand_sums[...])
    gathered = [tgt_finish(reduced[part], ITERS, part, jnp.log) for part in each]
    for part in each:
        for d in range(n_cand):
            if d:
                gathered[part][d - 1].wait_recv()
            out_tgt[of(part), z_columns(d)] = ag_slots[ITERS, part, d]
    for copy in pending:
        copy.wait_send()


def fused(candidates, targets, member, mix_weight):
    n_tgt, n_cand = lax.axis_size("tgt"), lax.axis_size("cand")
    rows, width = candidates.shape
    cols = targets.shape[0]
    mixes, tasks = mix_weight.shape
    share = cols // n_cand
    parts = 2 if mixes % 16 == 0 else 1
    group = mixes // parts
    return tuple(pl.pallas_call(
        functools.partial(fused_kernel, n_tgt, n_cand, parts),
        out_shape=(
            jax.ShapeDtypeStruct((mixes, rows), F32),
            jax.ShapeDtypeStruct((mixes, cols), F32),
        ),
        in_specs=[pl.BlockSpec(memory_space=pltpu.HBM)] * 2
        + [pl.BlockSpec(memory_space=pltpu.VMEM)] * 2,
        out_specs=(pl.BlockSpec(memory_space=pltpu.VMEM),) * 2,
        scratch_shapes=[
            pltpu.VMEM((rows, width), BF16),
            pltpu.VMEM((cols, width), BF16),
            pltpu.VMEM((cols, width), BF16),
            pltpu.VMEM((rows, cols), F32),
            pltpu.VMEM((rows, cols), BF16),
            pltpu.VMEM((rows, cols), BF16),
            pltpu.VMEM((mixes, cols), F32),
            pltpu.VMEM((mixes, rows), F32),
            pltpu.VMEM((n_tgt, 1, rows), F32),
            pltpu.VMEM((n_cand, 1, cols), F32),
            pltpu.VMEM((n_tgt, tasks, rows), F32),
            pltpu.VMEM((ITERS, parts, n_tgt, group, rows), F32),
            pltpu.VMEM((1 + ITERS, parts, n_cand - 1, group, share), F32),
            pltpu.VMEM((1 + ITERS, parts, n_cand, group, share), F32),
            pltpu.VMEM((1 + ITERS, parts, n_cand, group, share), F32),
            pltpu.SemaphoreType.DMA((2, max(rows, cols) // 256)),
            pltpu.SemaphoreType.DMA((2 + ITERS * parts, n_tgt - 1)),
            pltpu.SemaphoreType.DMA((2 + ITERS * parts, n_tgt - 1)),
            pltpu.SemaphoreType.DMA((1 + 2 * (1 + ITERS) * parts, n_cand - 1)),
            pltpu.SemaphoreType.DMA((1 + 2 * (1 + ITERS) * parts, n_cand - 1)),
        ],
        compiler_params=pltpu.CompilerParams(
            collective_id=0, has_side_effects=True, vmem_limit_bytes=56 * 1024 * 1024
        ),
    )(candidates, targets, member.reshape(1, -1), mix_weight))


def target_mass(own_member, member, mix_weight, cand_total):
    task_ids = jnp.arange(mix_weight.shape[1], dtype=jnp.int32)
    counts = jnp.sum((member[None, :] == task_ids[:, None]).astype(jnp.float32), axis=1)
    weight_total = jnp.dot(mix_weight, counts, precision=lax.Precision.HIGHEST)
    onehot = (own_member[None, :] == task_ids[:, None]).astype(jnp.float32)
    per_target = jnp.dot(mix_weight, onehot, precision=lax.Precision.HIGHEST)
    return per_target * (cand_total / weight_total)[:, None]


def by_collectives(candidates, targets, member, mix_weight):
    cand_rows = candidates.shape[0]
    tgt_rows = targets.shape[0]
    tgt_total = tgt_rows * lax.axis_size("tgt")
    cand_total = cand_rows * lax.axis_size("cand")
    tgt_unit = unit_rows(targets)
    scores = contract_last(unit_rows(candidates), tgt_unit)
    own_member = lax.dynamic_slice_in_dim(member, lax.axis_index("tgt") * tgt_rows, tgt_rows, 0)
    mass = target_mass(own_member, member, mix_weight, float(cand_total))
    kernel_one = jnp.exp(scores / EPS_FIRST) / tgt_total
    kernel_two = jnp.exp(scores / EPS_SECOND) / tgt_total
    scale_tgt = jnp.ones((mix_weight.shape[0], tgt_rows), jnp.float32)
    scale_cand = jnp.ones((mix_weight.shape[0], cand_rows), jnp.float32)
    for section_index, kernel in enumerate((kernel_one, kernel_two)):
        if section_index == 1:
            scale_tgt = scale_tgt * scale_tgt
        for repeat in range(ITERS):
            partial_value = lax.dot_general(
                scale_tgt, kernel, (((1,), (1,)), ((), ())), precision=lax.Precision.HIGHEST
            )
            scale_cand = 1.0 / lax.psum(partial_value, "tgt")
            column_part = jnp.dot(scale_cand, kernel, precision=lax.Precision.HIGHEST)
            share_cols = tgt_rows // lax.axis_size("cand")
            summed = lax.psum_scatter(column_part, "cand", scatter_dimension=1, tiled=True)
            own_mass = lax.dynamic_slice_in_dim(
                mass, lax.axis_index("cand") * share_cols, share_cols, 1
            )
            scale_tgt = lax.all_gather(own_mass / summed, "cand", axis=1, tiled=True)
    return (jnp.log(scale_cand), jnp.log(scale_tgt))


def solution(mesh):
    in_specs = (
        P(("groups", "cand"), None),
        P(("groups", "tgt"), None),
        P("groups"),
        P("mix", "groups"),
    )
    out_specs = (P("mix", ("groups", "cand")), P("mix", ("groups", "tgt")))
    n_tgt, n_cand = mesh.shape["tgt"], mesh.shape["cand"]

    def local(candidates, targets, member, mix_weight):
        lanes = targets.shape[0] % (128 * n_cand) == 0
        step = fused if lanes and n_cand > 1 and n_tgt > 1 else by_collectives
        return step(candidates, targets, member, mix_weight)

    return jax.shard_map(local, mesh=mesh, in_specs=in_specs, out_specs=out_specs, check_vma=False)
```

```python
import functools
import math

import jax
import jax.numpy as jnp
from jax import lax
from jax.experimental import pallas as pl
from jax.experimental.pallas import tpu as pltpu
from jax.sharding import PartitionSpec as P

ITERS = 2


EPS_FIRST = 0.05
EPS_SECOND = 0.025

MESH = pl.DeviceIdType.MESH
F32 = jnp.float32
BF16 = jnp.bfloat16
NT_DIMS = (((1,), (1,)), ((), ()))
TN_DIMS = (((0,), (0,)), ((), ()))
NN_DIMS = (((1,), (0,)), ((), ()))


def unit_rows(embedding):
    values = embedding.astype(jnp.float32)
    mean_sq = jnp.mean(values * values, axis=1, keepdims=True)
    return (values * (lax.rsqrt(mean_sq + 1e-06) * (1.0 / math.sqrt(values.shape[1])))).astype(
        jnp.bfloat16
    )


def contract_last(left, right):
    return lax.dot_general(left, right, NT_DIMS, preferred_element_type=jnp.float32)


def split_rows(value):
    head = value.astype(BF16)
    rest = (value - head.astype(F32)).astype(BF16)
    return jnp.concatenate([head, rest], axis=0)


def join_rows(value):
    half = value.shape[0] // 2
    return value[:half] + value[half:]


def fused_kernel(
    n_tgt, n_cand, parts, cand_hbm, tgt_hbm, member_ref, weight_ref, out_cand, out_tgt,
    cand_rows, tgt_rows, tgt_unit, raised, k_one, k_two, mass, cand_sums,
    row_slots, col_slots, task_slots, cand_slots, rs_send, rs_slots, ag_slots,
    load_sems, x_send, x_recv, z_send, z_recv, rs_out, rs_in, ag_out, ag_in,
):
    xi, zi = lax.axis_index("tgt"), lax.axis_index("cand")
    rows, width = cand_hbm.shape
    cols = tgt_hbm.shape[0]
    tasks, mixes = weight_ref.shape
    owners = (n_cand // 2 - 1, n_cand // 2)
    share = cols // len(owners)
    group = mixes // parts
    tgt_total, cand_total = cols * n_tgt, rows * n_cand
    block = 256

    def loads(src, dst, row):
        return [
            pltpu.make_async_copy(
                src.at[pl.ds(at, block)], dst.at[pl.ds(at, block)], load_sems.at[row, at // block]
            )
            for at in range(0, src.shape[0], block)
        ]

    tgt_loads, cand_loads = loads(tgt_hbm, tgt_rows, 0), loads(cand_hbm, cand_rows, 1)
    for copy in tgt_loads + cand_loads:
        copy.start()

    def x_peer(d):
        return {"tgt": lax.rem(xi + d, n_tgt)}

    def z_peer(d):
        return {"cand": lax.rem(zi + d, n_cand)}

    barrier = pltpu.get_barrier_semaphore()
    for d in range(1, n_tgt):
        pl.semaphore_signal(barrier, inc=1, device_id=x_peer(d), device_id_type=MESH)
    for d in range(1, n_cand):
        pl.semaphore_signal(barrier, inc=1, device_id=z_peer(d), device_id_type=MESH)

    pending = []
    xs, zs = (x_send, x_recv), (z_send, z_recv)

    def send(src, dst, sems, phase, d, peer):
        copy = pltpu.make_async_remote_copy(
            src_ref=src, dst_ref=dst,
            send_sem=sems[0].at[phase, d - 1], recv_sem=sems[1].at[phase, d - 1],
            device_id=peer, device_id_type=MESH,
        )
        copy.start()
        pending.append(copy)
        return copy

    def x_sum(slots):
        total = slots[lax.rem(xi + n_tgt, n_tgt)]
        for k in range(1, n_tgt):
            total = total + slots[lax.rem(xi - k + n_tgt, n_tgt)]
        return total

    def z_sum(slots):
        total = slots[lax.rem(zi + n_cand, n_cand)]
        for k in range(1, n_cand):
            total = total + slots[lax.rem(zi - k + n_cand, n_cand)]
        return total

    def x_start(slots, phase):
        return [send(slots.at[0], slots.at[d], xs, phase, d, x_peer(d)) for d in range(1, n_tgt)]

    def z_start(slots, phase):
        return [send(slots.at[0], slots.at[d], zs, phase, d, z_peer(d)) for d in range(1, n_cand)]

    def arrive(copies):
        for copy in copies:
            copy.wait_recv()

    all_ids = lax.broadcasted_iota(jnp.int32, (tasks, tgt_total), 0)
    all_hot = (member_ref[...] == all_ids).astype(F32)
    weights = weight_ref[...]
    per_target = lax.dot_general(
        weights, all_hot, TN_DIMS, precision=lax.Precision.HIGHEST, preferred_element_type=F32
    )
    ratio = float(cand_total) / jnp.sum(per_target, axis=1, keepdims=True)
    own = pl.ds(pl.multiple_of(xi * cols, cols), cols)
    own_hot = (
        member_ref[:, own] == lax.broadcasted_iota(jnp.int32, (tasks, cols), 0)
    ).astype(F32)
    mass[...] = (
        lax.dot_general(
            weights, own_hot, TN_DIMS, precision=lax.Precision.HIGHEST, preferred_element_type=F32
        )
        * ratio
    )

    for index, copy in enumerate(tgt_loads):
        copy.wait()
        at = pl.ds(index * block, block)
        tgt_unit[at, :] = unit_rows(tgt_rows[at, :])
    for copy in cand_loads:
        copy.wait()
    ones = jnp.ones((16, cols), BF16)
    for first in range(0, rows, block):
        at = pl.ds(first, block)
        scores = contract_last(unit_rows(cand_rows[at, :]), tgt_unit[...])
        power = jnp.exp(scores * (1.0 / EPS_FIRST))
        raised[at, :] = power
        kernel_rows = (power * (1.0 / tgt_total)).astype(BF16)
        k_one[at, :] = kernel_rows
        row_slots[0, :, at] = contract_last(ones, kernel_rows)[:1]

    def square(first, last):
        def step(b, carry):
            at = pl.ds(pl.multiple_of(b * 64, 64), 64)
            power = raised[at, :]
            k_two[at, :] = (power * power * (1.0 / tgt_total)).astype(BF16)
            return carry

        lax.fori_loop(first // 64, last // 64, step, 0)

    pl.semaphore_wait(barrier, n_tgt - 1 + n_cand - 1)

    copies = x_start(row_slots, 0)
    square(0, rows // 2)
    arrive(copies)
    scale_row = 1.0 / x_sum(row_slots)
    place = lax.broadcasted_iota(jnp.int32, (16, rows), 0)
    head = scale_row.astype(BF16).astype(F32)
    lhs = jnp.where(place == 0, head, jnp.where(place == 1, scale_row - head, 0.0)).astype(BF16)
    part = lax.dot_general(lhs, k_one[...], NN_DIMS, preferred_element_type=F32)
    col_slots[0] = part[:1] + part[1:2]
    copies = z_start(col_slots, 0)
    square(rows // 2, rows)
    arrive(copies)
    col_sum = z_sum(col_slots)

    task_slots[0] = join_rows(contract_last(split_rows(own_hot / col_sum), k_one[...]))
    arrive(x_start(task_slots, 1))
    cand_sums[...] = ratio * lax.dot_general(
        weights, x_sum(task_slots), TN_DIMS, precision=lax.Precision.HIGHEST,
        preferred_element_type=F32,
    )

    def of(part):
        return pl.ds(part * group, group)

    def half(o):
        return pl.ds(o * share, share)

    def to_owner(turn, part, o):
        return pltpu.make_async_remote_copy(
            src_ref=rs_send.at[turn, part, o], dst_ref=rs_slots.at[turn, part, zi],
            send_sem=rs_out.at[turn, part, o], recv_sem=rs_in.at[turn, part, zi],
            device_id={"cand": owners[o]}, device_id_type=MESH,
        )

    def from_owner(turn, part, o, peer):
        return pltpu.make_async_remote_copy(
            src_ref=ag_slots.at[turn, part, o], dst_ref=ag_slots.at[turn, part, o],
            send_sem=ag_out.at[turn, part, peer], recv_sem=ag_in.at[turn, part, o],
            device_id={"cand": peer}, device_id_type=MESH,
        )

    def owned_from(turn, part, o, source):
        return pltpu.make_async_remote_copy(
            src_ref=rs_send.at[turn, part, o], dst_ref=rs_slots.at[turn, part, source],
            send_sem=rs_out.at[turn, part, o], recv_sem=rs_in.at[turn, part, source],
            device_id={"cand": source}, device_id_type=MESH,
        )

    def others(o):
        return [z for z in range(n_cand) if z != owners[o]]

    halves = range(len(owners))

    def tgt_send(kernel, turn, part):
        lhs = split_rows(1.0 / cand_sums[of(part), :])
        for o in halves:
            value = join_rows(
                lax.dot_general(lhs, kernel[:, half(o)], NN_DIMS, preferred_element_type=F32)
            )
            rs_send[turn, part, o] = value

            @pl.when(zi != owners[o])
            def _():
                to_owner(turn, part, o).start()

    def tgt_finish(turn, part, change):
        for o in halves:

            @pl.when(zi == owners[o])
            def _():
                for z in others(o):
                    owned_from(turn, part, o, z).wait_recv()
                total = None
                for z in range(n_cand):
                    own = z == owners[o]
                    value = rs_send[turn, part, o] if own else rs_slots[turn, part, z]
                    total = value if total is None else total + value
                ag_slots[turn, part, o] = change(mass[of(part), half(o)] / total)
                for z in others(o):
                    from_owner(turn, part, o, z).start()

    def gathered(turn, part):
        for o in halves:

            @pl.when(zi != owners[o])
            def _():
                from_owner(turn, part, o, owners[o]).wait_recv()

    def drain(turn, part):
        for o in halves:

            @pl.when(zi != owners[o])
            def _():
                to_owner(turn, part, o).wait_send()

            @pl.when(zi == owners[o])
            def _():
                for z in others(o):
                    from_owner(turn, part, o, z).wait_send()

    def cand_send(turn, part):
        gathered(turn, part)
        total = None
        for o in halves:
            value = contract_last(split_rows(ag_slots[turn, part, o]), k_two[:, half(o)])
            total = value if total is None else total + value
        cand_slots[turn, part, 0] = join_rows(total)
        return x_start(cand_slots.at[turn, part], 2 + turn * parts + part)

    def cand_finish(copies, turn, part):
        arrive(copies)
        cand_sums[of(part), :] = x_sum(cand_slots.at[turn, part])

    def keep(scale):
        return scale

    each = range(parts)
    for part in each:
        tgt_send(k_one, 0, part)
    changes = (jnp.square,) + (keep,) * (ITERS - 1)
    for turn in range(ITERS):
        for part in each:
            tgt_finish(turn, part, changes[turn])
        summed = [cand_send(turn, part) for part in each]
        for part in each:
            cand_finish(summed[part], turn, part)
            tgt_send(k_two, 1 + turn, part)
    out_cand[...] = -jnp.log(cand_sums[...])
    for part in each:
        tgt_finish(ITERS, part, jnp.log)
    for part in each:
        gathered(ITERS, part)
        for o in halves:
            out_tgt[of(part), half(o)] = ag_slots[ITERS, part, o]
    for turn in range(1 + ITERS):
        for part in each:
            drain(turn, part)
    for copy in pending:
        copy.wait_send()


def fused(candidates, targets, member, mix_weight):
    n_tgt, n_cand = lax.axis_size("tgt"), lax.axis_size("cand")
    rows, width = candidates.shape
    cols = targets.shape[0]
    mixes, tasks = mix_weight.shape
    share = cols // 2
    parts = 2 if mixes % 16 == 0 else 1
    group = mixes // parts
    return tuple(pl.pallas_call(
        functools.partial(fused_kernel, n_tgt, n_cand, parts),
        out_shape=(
            jax.ShapeDtypeStruct((mixes, rows), F32),
            jax.ShapeDtypeStruct((mixes, cols), F32),
        ),
        in_specs=[pl.BlockSpec(memory_space=pltpu.HBM)] * 2
        + [pl.BlockSpec(memory_space=pltpu.VMEM)] * 2,
        out_specs=(pl.BlockSpec(memory_space=pltpu.VMEM),) * 2,
        scratch_shapes=[
            pltpu.VMEM((rows, width), BF16),
            pltpu.VMEM((cols, width), BF16),
            pltpu.VMEM((cols, width), BF16),
            pltpu.VMEM((rows, cols), F32),
            pltpu.VMEM((rows, cols), BF16),
            pltpu.VMEM((rows, cols), BF16),
            pltpu.VMEM((mixes, cols), F32),
            pltpu.VMEM((mixes, rows), F32),
            pltpu.VMEM((n_tgt, 1, rows), F32),
            pltpu.VMEM((n_cand, 1, cols), F32),
            pltpu.VMEM((n_tgt, tasks, rows), F32),
            pltpu.VMEM((ITERS, parts, n_tgt, group, rows), F32),
            pltpu.VMEM((1 + ITERS, parts, 2, group, share), F32),
            pltpu.VMEM((1 + ITERS, parts, n_cand, group, share), F32),
            pltpu.VMEM((1 + ITERS, parts, 2, group, share), F32),
            pltpu.SemaphoreType.DMA((2, max(rows, cols) // 256)),
            pltpu.SemaphoreType.DMA((2 + ITERS * parts, n_tgt - 1)),
            pltpu.SemaphoreType.DMA((2 + ITERS * parts, n_tgt - 1)),
            pltpu.SemaphoreType.DMA((1, n_cand - 1)),
            pltpu.SemaphoreType.DMA((1, n_cand - 1)),
            pltpu.SemaphoreType.DMA((1 + ITERS, parts, 2)),
            pltpu.SemaphoreType.DMA((1 + ITERS, parts, n_cand)),
            pltpu.SemaphoreType.DMA((1 + ITERS, parts, n_cand)),
            pltpu.SemaphoreType.DMA((1 + ITERS, parts, 2)),
        ],
        compiler_params=pltpu.CompilerParams(
            collective_id=0, has_side_effects=True, vmem_limit_bytes=56 * 1024 * 1024
        ),
    )(candidates, targets, member.reshape(1, -1), mix_weight.T))


def target_mass(own_member, member, mix_weight, cand_total):
    task_ids = jnp.arange(mix_weight.shape[1], dtype=jnp.int32)
    counts = jnp.sum((member[None, :] == task_ids[:, None]).astype(jnp.float32), axis=1)
    weight_total = jnp.dot(mix_weight, counts, precision=lax.Precision.HIGHEST)
    onehot = (own_member[None, :] == task_ids[:, None]).astype(jnp.float32)
    per_target = jnp.dot(mix_weight, onehot, precision=lax.Precision.HIGHEST)
    return per_target * (cand_total / weight_total)[:, None]


def by_collectives(candidates, targets, member, mix_weight):
    cand_rows = candidates.shape[0]
    tgt_rows = targets.shape[0]
    tgt_total = tgt_rows * lax.axis_size("tgt")
    cand_total = cand_rows * lax.axis_size("cand")
    tgt_unit = unit_rows(targets)
    scores = contract_last(unit_rows(candidates), tgt_unit)
    own_member = lax.dynamic_slice_in_dim(member, lax.axis_index("tgt") * tgt_rows, tgt_rows, 0)
    mass = target_mass(own_member, member, mix_weight, float(cand_total))
    kernel_one = jnp.exp(scores / EPS_FIRST) / tgt_total
    kernel_two = jnp.exp(scores / EPS_SECOND) / tgt_total
    scale_tgt = jnp.ones((mix_weight.shape[0], tgt_rows), jnp.float32)
    scale_cand = jnp.ones((mix_weight.shape[0], cand_rows), jnp.float32)
    for section_index, kernel in enumerate((kernel_one, kernel_two)):
        if section_index == 1:
            scale_tgt = scale_tgt * scale_tgt
        for repeat in range(ITERS):
            partial_value = lax.dot_general(
                scale_tgt, kernel, (((1,), (1,)), ((), ())), precision=lax.Precision.HIGHEST
            )
            scale_cand = 1.0 / lax.psum(partial_value, "tgt")
            column_part = jnp.dot(scale_cand, kernel, precision=lax.Precision.HIGHEST)
            share_cols = tgt_rows // lax.axis_size("cand")
            summed = lax.psum_scatter(column_part, "cand", scatter_dimension=1, tiled=True)
            own_mass = lax.dynamic_slice_in_dim(
                mass, lax.axis_index("cand") * share_cols, share_cols, 1
            )
            scale_tgt = lax.all_gather(own_mass / summed, "cand", axis=1, tiled=True)
    return (jnp.log(scale_cand), jnp.log(scale_tgt))


def solution(mesh):
    in_specs = (
        P(("groups", "cand"), None),
        P(("groups", "tgt"), None),
        P("groups"),
        P("mix", "groups"),
    )
    out_specs = (P("mix", ("groups", "cand")), P("mix", ("groups", "tgt")))
    n_tgt, n_cand = mesh.shape["tgt"], mesh.shape["cand"]

    def local(candidates, targets, member, mix_weight):
        lanes = targets.shape[0] % (128 * n_cand) == 0 and candidates.shape[0] % 256 == 0
        step = fused if lanes and n_cand > 1 and n_tgt > 1 else by_collectives
        return step(candidates, targets, member, mix_weight)

    return jax.shard_map(local, mesh=mesh, in_specs=in_specs, out_specs=out_specs, check_vma=False)
```

```python
import functools
import math

import jax
import jax.numpy as jnp
from jax import lax
from jax.experimental import pallas as pl
from jax.experimental.pallas import tpu as pltpu
from jax.sharding import PartitionSpec as P

ITERS = 2


EPS_FIRST = 0.05
EPS_SECOND = 0.025

MESH = pl.DeviceIdType.MESH
F32 = jnp.float32
BF16 = jnp.bfloat16
NT_DIMS = (((1,), (1,)), ((), ()))
TN_DIMS = (((0,), (0,)), ((), ()))
NN_DIMS = (((1,), (0,)), ((), ()))


def unit_rows(embedding):
    values = embedding.astype(jnp.float32)
    mean_sq = jnp.mean(values * values, axis=1, keepdims=True)
    return (values * (lax.rsqrt(mean_sq + 1e-06) * (1.0 / math.sqrt(values.shape[1])))).astype(
        jnp.bfloat16
    )


def contract_last(left, right):
    return lax.dot_general(left, right, NT_DIMS, preferred_element_type=jnp.float32)


def split_rows(value):
    head = value.astype(BF16)
    rest = (value - head.astype(F32)).astype(BF16)
    return jnp.concatenate([head, rest], axis=0)


def join_rows(value):
    half = value.shape[0] // 2
    return value[:half] + value[half:]


def fused_kernel(
    n_tgt, n_cand, n_mix, parts, cand_hbm, tgt_hbm, member_ref, weight_ref, out_cand, out_tgt,
    cand_rows, tgt_rows, tgt_unit, raised, k_one, k_two, mass, cand_sums,
    row_part, row_slots, col_slots, task_slots, cand_slots, rs_send, rs_slots, ag_slots,
    load_sems, x_send, x_recv, z_send, z_recv, row_out, row_in, rs_out, rs_in, ag_out, ag_in,
):
    xi, zi, ci = lax.axis_index("tgt"), lax.axis_index("cand"), lax.axis_index("mix")
    rows, width = cand_hbm.shape
    cols = tgt_hbm.shape[0]
    tasks, mixes = weight_ref.shape
    owners = (n_cand // 2 - 1, n_cand // 2)
    share = cols // len(owners)
    group = mixes // parts
    tgt_total, cand_total = cols * n_tgt, rows * n_cand
    block = 256

    def loads(src, dst, row):
        return [
            pltpu.make_async_copy(
                src.at[pl.ds(at, block)], dst.at[pl.ds(at, block)], load_sems.at[row, at // block]
            )
            for at in range(0, src.shape[0], block)
        ]

    tgt_loads, cand_loads = loads(tgt_hbm, tgt_rows, 0), loads(cand_hbm, cand_rows, 1)
    for copy in tgt_loads + cand_loads:
        copy.start()

    def x_peer(d):
        return {"tgt": lax.rem(xi + d, n_tgt)}

    def xc_peer(d, e):
        return {"tgt": lax.rem(xi + d, n_tgt), "mix": lax.rem(ci + e, n_mix)}

    def z_peer(d):
        return {"cand": lax.rem(zi + d, n_cand)}

    barrier = pltpu.get_barrier_semaphore()
    for d in range(1, n_tgt):
        for e in range(n_mix):
            pl.semaphore_signal(barrier, inc=1, device_id=xc_peer(d, e), device_id_type=MESH)
    for d in range(1, n_cand):
        pl.semaphore_signal(barrier, inc=1, device_id=z_peer(d), device_id_type=MESH)

    pending = []
    xs, zs = (x_send, x_recv), (z_send, z_recv)

    def send(src, dst, sems, phase, d, peer):
        copy = pltpu.make_async_remote_copy(
            src_ref=src, dst_ref=dst,
            send_sem=sems[0].at[phase, d - 1], recv_sem=sems[1].at[phase, d - 1],
            device_id=peer, device_id_type=MESH,
        )
        copy.start()
        pending.append(copy)
        return copy

    def x_sum(slots):
        total = slots[lax.rem(xi + n_tgt, n_tgt)]
        for k in range(1, n_tgt):
            total = total + slots[lax.rem(xi - k + n_tgt, n_tgt)]
        return total

    def z_sum(slots):
        total = slots[lax.rem(zi + n_cand, n_cand)]
        for k in range(1, n_cand):
            total = total + slots[lax.rem(zi - k + n_cand, n_cand)]
        return total

    def x_start(slots, phase):
        return [send(slots.at[0], slots.at[d], xs, phase, d, x_peer(d)) for d in range(1, n_tgt)]

    def z_start(slots, phase):
        return [send(slots.at[0], slots.at[d], zs, phase, d, z_peer(d)) for d in range(1, n_cand)]

    def arrive(copies):
        for copy in copies:
            copy.wait_recv()

    all_ids = lax.broadcasted_iota(jnp.int32, (tasks, tgt_total), 0)
    all_hot = (member_ref[...] == all_ids).astype(F32)
    weights = weight_ref[...]
    per_target = lax.dot_general(
        weights, all_hot, TN_DIMS, precision=lax.Precision.HIGHEST, preferred_element_type=F32
    )
    ratio = float(cand_total) / jnp.sum(per_target, axis=1, keepdims=True)
    own = pl.ds(pl.multiple_of(xi * cols, cols), cols)
    own_hot = (
        member_ref[:, own] == lax.broadcasted_iota(jnp.int32, (tasks, cols), 0)
    ).astype(F32)
    mass[...] = (
        lax.dot_general(
            weights, own_hot, TN_DIMS, precision=lax.Precision.HIGHEST, preferred_element_type=F32
        )
        * ratio
    )

    for index, copy in enumerate(tgt_loads):
        copy.wait()
        at = pl.ds(index * block, block)
        tgt_unit[at, :] = unit_rows(tgt_rows[at, :])
    for copy in cand_loads:
        copy.wait()
    ones = jnp.ones((16, cols), BF16)
    early = rows // n_mix

    def build(first):
        at = pl.ds(pl.multiple_of(first, block), block)
        scores = contract_last(unit_rows(cand_rows[at, :]), tgt_unit[...])
        power = jnp.exp(scores * (1.0 / EPS_FIRST))
        raised[at, :] = power
        kernel_rows = (power * (1.0 / tgt_total)).astype(BF16)
        k_one[at, :] = kernel_rows
        return contract_last(ones, kernel_rows)[:1]

    for first in range(0, early, block):
        row_part[ci, :, pl.ds(first, block)] = build(ci * early + first)
    pl.semaphore_wait(barrier, (n_tgt - 1) * n_mix + n_cand - 1)
    row_copies = []
    for d in range(1, n_tgt):
        for e in range(n_mix):
            row_copies.append(pltpu.make_async_remote_copy(
                src_ref=row_part.at[ci], dst_ref=row_slots.at[d, ci],
                send_sem=row_out.at[d - 1, e], recv_sem=row_in.at[d - 1, ci],
                device_id=xc_peer(d, e), device_id_type=MESH,
            ))
            row_copies[-1].start()
    for later in range(1, n_mix):
        other = lax.rem(ci + later, n_mix)
        for first in range(0, early, block):
            row_part[other, :, pl.ds(first, block)] = build(other * early + first)

    def square(first, last):
        def step(b, carry):
            at = pl.ds(pl.multiple_of(b * 64, 64), 64)
            power = raised[at, :]
            k_two[at, :] = (power * power * (1.0 / tgt_total)).astype(BF16)
            return carry

        lax.fori_loop(first // 64, last // 64, step, 0)


    square(0, rows // 2)
    for d in range(1, n_tgt):
        for e in range(n_mix):
            pltpu.make_async_remote_copy(
                src_ref=row_part.at[e], dst_ref=row_slots.at[d, e],
                send_sem=row_out.at[d - 1, e], recv_sem=row_in.at[d - 1, e],
                device_id=x_peer(d), device_id_type=MESH,
            ).wait_recv()
    row_sums = []
    for e in range(n_mix):
        value = row_part[e]
        for d in range(1, n_tgt):
            value = value + row_slots[d, e]
        row_sums.append(value)
    scale_row = 1.0 / jnp.concatenate(row_sums, axis=1)
    place = lax.broadcasted_iota(jnp.int32, (16, rows), 0)
    head = scale_row.astype(BF16).astype(F32)
    lhs = jnp.where(place == 0, head, jnp.where(place == 1, scale_row - head, 0.0)).astype(BF16)
    part = lax.dot_general(lhs, k_one[...], NN_DIMS, preferred_element_type=F32)
    col_slots[0] = part[:1] + part[1:2]
    copies = z_start(col_slots, 0)
    square(rows // 2, rows)
    arrive(copies)
    col_sum = z_sum(col_slots)

    task_slots[0] = join_rows(contract_last(split_rows(own_hot / col_sum), k_one[...]))
    arrive(x_start(task_slots, 1))
    cand_sums[...] = ratio * lax.dot_general(
        weights, x_sum(task_slots), TN_DIMS, precision=lax.Precision.HIGHEST,
        preferred_element_type=F32,
    )

    def of(part):
        return pl.ds(part * group, group)

    def half(o):
        return pl.ds(o * share, share)

    def to_owner(turn, part, o):
        return pltpu.make_async_remote_copy(
            src_ref=rs_send.at[turn, part, o], dst_ref=rs_slots.at[turn, part, zi],
            send_sem=rs_out.at[turn, part, o], recv_sem=rs_in.at[turn, part, zi],
            device_id={"cand": owners[o]}, device_id_type=MESH,
        )

    def from_owner(turn, part, o, peer):
        return pltpu.make_async_remote_copy(
            src_ref=ag_slots.at[turn, part, o], dst_ref=ag_slots.at[turn, part, o],
            send_sem=ag_out.at[turn, part, peer], recv_sem=ag_in.at[turn, part, o],
            device_id={"cand": peer}, device_id_type=MESH,
        )

    def owned_from(turn, part, o, source):
        return pltpu.make_async_remote_copy(
            src_ref=rs_send.at[turn, part, o], dst_ref=rs_slots.at[turn, part, source],
            send_sem=rs_out.at[turn, part, o], recv_sem=rs_in.at[turn, part, source],
            device_id={"cand": source}, device_id_type=MESH,
        )

    def others(o):
        return [z for z in range(n_cand) if z != owners[o]]

    halves = range(len(owners))

    def tgt_send(kernel, turn, part):
        lhs = split_rows(1.0 / cand_sums[of(part), :])
        for o in halves:
            value = join_rows(
                lax.dot_general(lhs, kernel[:, half(o)], NN_DIMS, preferred_element_type=F32)
            )
            rs_send[turn, part, o] = value

            @pl.when(zi != owners[o])
            def _():
                to_owner(turn, part, o).start()

    def tgt_finish(turn, part, change):
        for o in halves:

            @pl.when(zi == owners[o])
            def _():
                for z in others(o):
                    owned_from(turn, part, o, z).wait_recv()
                total = None
                for z in range(n_cand):
                    own = z == owners[o]
                    value = rs_send[turn, part, o] if own else rs_slots[turn, part, z]
                    total = value if total is None else total + value
                ag_slots[turn, part, o] = change(mass[of(part), half(o)] / total)
                for z in others(o):
                    from_owner(turn, part, o, z).start()

    def gathered(turn, part):
        for o in halves:

            @pl.when(zi != owners[o])
            def _():
                from_owner(turn, part, o, owners[o]).wait_recv()

    def drain(turn, part):
        for o in halves:

            @pl.when(zi != owners[o])
            def _():
                to_owner(turn, part, o).wait_send()

            @pl.when(zi == owners[o])
            def _():
                for z in others(o):
                    from_owner(turn, part, o, z).wait_send()

    def cand_send(turn, part):
        gathered(turn, part)
        total = None
        for o in halves:
            value = contract_last(split_rows(ag_slots[turn, part, o]), k_two[:, half(o)])
            total = value if total is None else total + value
        cand_slots[turn, part, 0] = join_rows(total)
        return x_start(cand_slots.at[turn, part], 2 + turn * parts + part)

    def cand_finish(copies, turn, part):
        arrive(copies)
        cand_sums[of(part), :] = x_sum(cand_slots.at[turn, part])

    def keep(scale):
        return scale

    each = range(parts)
    for part in each:
        tgt_send(k_one, 0, part)
    changes = (jnp.square,) + (keep,) * (ITERS - 1)
    for turn in range(ITERS):
        for part in each:
            tgt_finish(turn, part, changes[turn])
        summed = [cand_send(turn, part) for part in each]
        for part in each:
            cand_finish(summed[part], turn, part)
            tgt_send(k_two, 1 + turn, part)
    out_cand[...] = -jnp.log(cand_sums[...])
    for part in each:
        tgt_finish(ITERS, part, jnp.log)
    for part in each:
        gathered(ITERS, part)
        for o in halves:
            out_tgt[of(part), half(o)] = ag_slots[ITERS, part, o]
    for turn in range(1 + ITERS):
        for part in each:
            drain(turn, part)
    for copy in pending + row_copies:
        copy.wait_send()


def fused(candidates, targets, member, mix_weight):
    n_tgt, n_cand = lax.axis_size("tgt"), lax.axis_size("cand")
    rows, width = candidates.shape
    cols = targets.shape[0]
    mixes, tasks = mix_weight.shape
    n_mix = lax.axis_size("mix")
    share = cols // 2
    parts = 2 if mixes % 16 == 0 else 1
    group = mixes // parts
    return tuple(pl.pallas_call(
        functools.partial(fused_kernel, n_tgt, n_cand, n_mix, parts),
        out_shape=(
            jax.ShapeDtypeStruct((mixes, rows), F32),
            jax.ShapeDtypeStruct((mixes, cols), F32),
        ),
        in_specs=[pl.BlockSpec(memory_space=pltpu.HBM)] * 2
        + [pl.BlockSpec(memory_space=pltpu.VMEM)] * 2,
        out_specs=(pl.BlockSpec(memory_space=pltpu.VMEM),) * 2,
        scratch_shapes=[
            pltpu.VMEM((rows, width), BF16),
            pltpu.VMEM((cols, width), BF16),
            pltpu.VMEM((cols, width), BF16),
            pltpu.VMEM((rows, cols), F32),
            pltpu.VMEM((rows, cols), BF16),
            pltpu.VMEM((rows, cols), BF16),
            pltpu.VMEM((mixes, cols), F32),
            pltpu.VMEM((mixes, rows), F32),
            pltpu.VMEM((n_mix, 1, rows // n_mix), F32),
            pltpu.VMEM((n_tgt, n_mix, 1, rows // n_mix), F32),
            pltpu.VMEM((n_cand, 1, cols), F32),
            pltpu.VMEM((n_tgt, tasks, rows), F32),
            pltpu.VMEM((ITERS, parts, n_tgt, group, rows), F32),
            pltpu.VMEM((1 + ITERS, parts, 2, group, share), F32),
            pltpu.VMEM((1 + ITERS, parts, n_cand, group, share), F32),
            pltpu.VMEM((1 + ITERS, parts, 2, group, share), F32),
            pltpu.SemaphoreType.DMA((2, max(rows, cols) // 256)),
            pltpu.SemaphoreType.DMA((2 + ITERS * parts, n_tgt - 1)),
            pltpu.SemaphoreType.DMA((2 + ITERS * parts, n_tgt - 1)),
            pltpu.SemaphoreType.DMA((1, n_cand - 1)),
            pltpu.SemaphoreType.DMA((1, n_cand - 1)),
            pltpu.SemaphoreType.DMA((n_tgt - 1, n_mix)),
            pltpu.SemaphoreType.DMA((n_tgt - 1, n_mix)),
            pltpu.SemaphoreType.DMA((1 + ITERS, parts, 2)),
            pltpu.SemaphoreType.DMA((1 + ITERS, parts, n_cand)),
            pltpu.SemaphoreType.DMA((1 + ITERS, parts, n_cand)),
            pltpu.SemaphoreType.DMA((1 + ITERS, parts, 2)),
        ],
        compiler_params=pltpu.CompilerParams(
            collective_id=0, has_side_effects=True, vmem_limit_bytes=56 * 1024 * 1024
        ),
    )(candidates, targets, member.reshape(1, -1), mix_weight.T))


def target_mass(own_member, member, mix_weight, cand_total):
    task_ids = jnp.arange(mix_weight.shape[1], dtype=jnp.int32)
    counts = jnp.sum((member[None, :] == task_ids[:, None]).astype(jnp.float32), axis=1)
    weight_total = jnp.dot(mix_weight, counts, precision=lax.Precision.HIGHEST)
    onehot = (own_member[None, :] == task_ids[:, None]).astype(jnp.float32)
    per_target = jnp.dot(mix_weight, onehot, precision=lax.Precision.HIGHEST)
    return per_target * (cand_total / weight_total)[:, None]


def by_collectives(candidates, targets, member, mix_weight):
    cand_rows = candidates.shape[0]
    tgt_rows = targets.shape[0]
    tgt_total = tgt_rows * lax.axis_size("tgt")
    cand_total = cand_rows * lax.axis_size("cand")
    tgt_unit = unit_rows(targets)
    scores = contract_last(unit_rows(candidates), tgt_unit)
    own_member = lax.dynamic_slice_in_dim(member, lax.axis_index("tgt") * tgt_rows, tgt_rows, 0)
    mass = target_mass(own_member, member, mix_weight, float(cand_total))
    kernel_one = jnp.exp(scores / EPS_FIRST) / tgt_total
    kernel_two = jnp.exp(scores / EPS_SECOND) / tgt_total
    scale_tgt = jnp.ones((mix_weight.shape[0], tgt_rows), jnp.float32)
    scale_cand = jnp.ones((mix_weight.shape[0], cand_rows), jnp.float32)
    for section_index, kernel in enumerate((kernel_one, kernel_two)):
        if section_index == 1:
            scale_tgt = scale_tgt * scale_tgt
        for repeat in range(ITERS):
            partial_value = lax.dot_general(
                scale_tgt, kernel, (((1,), (1,)), ((), ())), precision=lax.Precision.HIGHEST
            )
            scale_cand = 1.0 / lax.psum(partial_value, "tgt")
            column_part = jnp.dot(scale_cand, kernel, precision=lax.Precision.HIGHEST)
            share_cols = tgt_rows // lax.axis_size("cand")
            summed = lax.psum_scatter(column_part, "cand", scatter_dimension=1, tiled=True)
            own_mass = lax.dynamic_slice_in_dim(
                mass, lax.axis_index("cand") * share_cols, share_cols, 1
            )
            scale_tgt = lax.all_gather(own_mass / summed, "cand", axis=1, tiled=True)
    return (jnp.log(scale_cand), jnp.log(scale_tgt))


def solution(mesh):
    in_specs = (
        P(("groups", "cand"), None),
        P(("groups", "tgt"), None),
        P("groups"),
        P("mix", "groups"),
    )
    out_specs = (P("mix", ("groups", "cand")), P("mix", ("groups", "tgt")))
    n_tgt, n_cand = mesh.shape["tgt"], mesh.shape["cand"]

    def local(candidates, targets, member, mix_weight):
        lanes = targets.shape[0] % (128 * n_cand) == 0 and candidates.shape[0] % 512 == 0
        step = fused if lanes and n_cand > 1 and n_tgt > 1 else by_collectives
        return step(candidates, targets, member, mix_weight)

    return jax.shard_map(local, mesh=mesh, in_specs=in_specs, out_specs=out_specs, check_vma=False)
```

```python
import functools
import math

import jax
import jax.numpy as jnp
from jax import lax
from jax.experimental import pallas as pl
from jax.experimental.pallas import tpu as pltpu
from jax.sharding import PartitionSpec as P

ITERS = 2


EPS_FIRST = 0.05
EPS_SECOND = 0.025

MESH = pl.DeviceIdType.MESH
F32 = jnp.float32
BF16 = jnp.bfloat16
NT_DIMS = (((1,), (1,)), ((), ()))
TN_DIMS = (((0,), (0,)), ((), ()))
NN_DIMS = (((1,), (0,)), ((), ()))


def unit_rows(embedding):
    values = embedding.astype(jnp.float32)
    mean_sq = jnp.mean(values * values, axis=1, keepdims=True)
    return (values * (lax.rsqrt(mean_sq + 1e-06) * (1.0 / math.sqrt(values.shape[1])))).astype(
        jnp.bfloat16
    )


def contract_last(left, right):
    return lax.dot_general(left, right, NT_DIMS, preferred_element_type=jnp.float32)


def split_rows(value):
    head = value.astype(BF16)
    rest = (value - head.astype(F32)).astype(BF16)
    return jnp.concatenate([head, rest], axis=0)


def join_rows(value):
    half = value.shape[0] // 2
    return value[:half] + value[half:]


def fused_kernel(
    n_tgt, n_cand, n_mix, parts, cand_hbm, tgt_hbm, member_ref, weight_ref, out_cand, out_tgt,
    cand_rows, tgt_rows, tgt_unit, raised, k_one, k_two, mass, cand_sums,
    row_part, row_slots, col_slots, task_slots, cand_slots, rs_send, rs_slots, ag_slots,
    load_sems, x_send, x_recv, z_send, z_recv, row_out, row_in, rs_out, rs_in, ag_out, ag_in,
):
    xi, zi, ci = lax.axis_index("tgt"), lax.axis_index("cand"), lax.axis_index("mix")
    rows, width = cand_hbm.shape
    cols = tgt_hbm.shape[0]
    tasks, mixes = weight_ref.shape
    owners = (n_cand // 2 - 1, n_cand // 2)
    share = cols // len(owners)
    group = mixes // parts
    tgt_total, cand_total = cols * n_tgt, rows * n_cand
    block = 256

    def loads(src, dst, row):
        return [
            pltpu.make_async_copy(
                src.at[pl.ds(at, block)], dst.at[pl.ds(at, block)], load_sems.at[row, at // block]
            )
            for at in range(0, src.shape[0], block)
        ]

    tgt_loads, cand_loads = loads(tgt_hbm, tgt_rows, 0), loads(cand_hbm, cand_rows, 1)
    for copy in tgt_loads + cand_loads:
        copy.start()

    def x_peer(d):
        return {"tgt": lax.rem(xi + d, n_tgt)}

    def xc_peer(d, e):
        return {"tgt": lax.rem(xi + d, n_tgt), "mix": lax.rem(ci + e, n_mix)}

    def z_peer(d):
        return {"cand": lax.rem(zi + d, n_cand)}

    barrier = pltpu.get_barrier_semaphore()
    for d in range(1, n_tgt):
        for e in range(n_mix):
            pl.semaphore_signal(barrier, inc=1, device_id=xc_peer(d, e), device_id_type=MESH)
    for d in range(1, n_cand):
        pl.semaphore_signal(barrier, inc=1, device_id=z_peer(d), device_id_type=MESH)

    pending = []
    xs, zs = (x_send, x_recv), (z_send, z_recv)

    def send(src, dst, sems, phase, d, peer):
        copy = pltpu.make_async_remote_copy(
            src_ref=src, dst_ref=dst,
            send_sem=sems[0].at[phase, d - 1], recv_sem=sems[1].at[phase, d - 1],
            device_id=peer, device_id_type=MESH,
        )
        copy.start()
        pending.append(copy)
        return copy

    def x_sum(slots):
        total = slots[lax.rem(xi + n_tgt, n_tgt)]
        for k in range(1, n_tgt):
            total = total + slots[lax.rem(xi - k + n_tgt, n_tgt)]
        return total

    def z_sum(slots):
        total = slots[lax.rem(zi + n_cand, n_cand)]
        for k in range(1, n_cand):
            total = total + slots[lax.rem(zi - k + n_cand, n_cand)]
        return total

    def x_start(slots, phase):
        return [send(slots.at[0], slots.at[d], xs, phase, d, x_peer(d)) for d in range(1, n_tgt)]

    def z_start(slots, phase):
        return [send(slots.at[0], slots.at[d], zs, phase, d, z_peer(d)) for d in range(1, n_cand)]

    def arrive(copies):
        for copy in copies:
            copy.wait_recv()

    all_ids = lax.broadcasted_iota(jnp.int32, (tasks, tgt_total), 0)
    all_hot = (member_ref[...] == all_ids).astype(F32)
    weights = weight_ref[...]
    per_target = lax.dot_general(
        weights, all_hot, TN_DIMS, precision=lax.Precision.HIGHEST, preferred_element_type=F32
    )
    ratio = float(cand_total) / jnp.sum(per_target, axis=1, keepdims=True)
    own = pl.ds(pl.multiple_of(xi * cols, cols), cols)
    own_hot = (
        member_ref[:, own] == lax.broadcasted_iota(jnp.int32, (tasks, cols), 0)
    ).astype(F32)
    mass[...] = (
        lax.dot_general(
            weights, own_hot, TN_DIMS, precision=lax.Precision.HIGHEST, preferred_element_type=F32
        )
        * ratio
    )

    for index, copy in enumerate(tgt_loads):
        copy.wait()
        at = pl.ds(index * block, block)
        tgt_unit[at, :] = unit_rows(tgt_rows[at, :])
    for copy in cand_loads:
        copy.wait()
    ones = jnp.ones((16, cols), BF16)
    early = rows // n_mix

    def build(first):
        at = pl.ds(pl.multiple_of(first, block), block)
        scores = contract_last(unit_rows(cand_rows[at, :]), tgt_unit[...])
        power = jnp.exp(scores * (1.0 / EPS_FIRST))
        raised[at, :] = power
        kernel_rows = (power * (1.0 / tgt_total)).astype(BF16)
        k_one[at, :] = kernel_rows
        return contract_last(ones, kernel_rows)[:1]

    for first in range(0, early, block):
        row_part[ci, :, pl.ds(first, block)] = build(ci * early + first)
    pl.semaphore_wait(barrier, (n_tgt - 1) * n_mix + n_cand - 1)
    row_copies = []
    for d in range(1, n_tgt):
        for e in range(n_mix):
            row_copies.append(pltpu.make_async_remote_copy(
                src_ref=row_part.at[ci], dst_ref=row_slots.at[d, ci],
                send_sem=row_out.at[d - 1, e], recv_sem=row_in.at[d - 1, ci],
                device_id=xc_peer(d, e), device_id_type=MESH,
            ))
            row_copies[-1].start()
    for later in range(1, n_mix):
        other = lax.rem(ci + later, n_mix)
        for first in range(0, early, block):
            row_part[other, :, pl.ds(first, block)] = build(other * early + first)

    def square(first, last):
        def step(b, carry):
            at = pl.ds(pl.multiple_of(b * 64, 64), 64)
            power = raised[at, :]
            k_two[at, :] = (power * power * (1.0 / tgt_total)).astype(BF16)
            return carry

        lax.fori_loop(first // 64, last // 64, step, 0)


    for d in range(1, n_tgt):
        for e in range(n_mix):
            pltpu.make_async_remote_copy(
                src_ref=row_part.at[e], dst_ref=row_slots.at[d, e],
                send_sem=row_out.at[d - 1, e], recv_sem=row_in.at[d - 1, e],
                device_id=x_peer(d), device_id_type=MESH,
            ).wait_recv()
    row_sums = []
    for e in range(n_mix):
        value = row_part[e]
        for d in range(1, n_tgt):
            value = value + row_slots[d, e]
        row_sums.append(value)
    scale_row = 1.0 / jnp.concatenate(row_sums, axis=1)
    place = lax.broadcasted_iota(jnp.int32, (16, rows), 0)
    head = scale_row.astype(BF16).astype(F32)
    lhs = jnp.where(place == 0, head, jnp.where(place == 1, scale_row - head, 0.0)).astype(BF16)
    part = lax.dot_general(lhs, k_one[...], NN_DIMS, preferred_element_type=F32)
    col_slots[0] = part[:1] + part[1:2]
    copies = z_start(col_slots, 0)
    square(0, rows)
    arrive(copies)
    col_sum = z_sum(col_slots)

    task_slots[0] = join_rows(contract_last(split_rows(own_hot / col_sum), k_one[...]))
    arrive(x_start(task_slots, 1))
    cand_sums[...] = ratio * lax.dot_general(
        weights, x_sum(task_slots), TN_DIMS, precision=lax.Precision.HIGHEST,
        preferred_element_type=F32,
    )

    def of(part):
        return pl.ds(part * group, group)

    def half(o):
        return pl.ds(o * share if isinstance(o, int) else pl.multiple_of(o * share, share), share)

    far = 1 - zi // owners[1]
    near = 1 - far

    def to_owner(turn, part, o):
        return pltpu.make_async_remote_copy(
            src_ref=rs_send.at[turn, part, o], dst_ref=rs_slots.at[turn, part, zi],
            send_sem=rs_out.at[turn, part, o], recv_sem=rs_in.at[turn, part, zi],
            device_id={"cand": owners[0] + o}, device_id_type=MESH,
        )

    def from_owner(turn, part, o, peer):
        return pltpu.make_async_remote_copy(
            src_ref=ag_slots.at[turn, part, o], dst_ref=ag_slots.at[turn, part, o],
            send_sem=ag_out.at[turn, part, peer], recv_sem=ag_in.at[turn, part, o],
            device_id={"cand": peer}, device_id_type=MESH,
        )

    def owned_from(turn, part, o, source):
        return pltpu.make_async_remote_copy(
            src_ref=rs_send.at[turn, part, o], dst_ref=rs_slots.at[turn, part, source],
            send_sem=rs_out.at[turn, part, o], recv_sem=rs_in.at[turn, part, source],
            device_id={"cand": source}, device_id_type=MESH,
        )

    def others(o):
        return [z for z in range(n_cand) if z != owners[o]]

    halves = range(len(owners))

    def tgt_send(kernel, turn, part):
        lhs = split_rows(1.0 / cand_sums[of(part), :])
        for o in (far, near):
            rs_send[turn, part, o] = join_rows(
                lax.dot_general(lhs, kernel[:, half(o)], NN_DIMS, preferred_element_type=F32)
            )
            if o is far:
                to_owner(turn, part, o).start()
                continue

            @pl.when(zi != owners[0] + o)
            def _():
                to_owner(turn, part, o).start()

    def tgt_finish(turn, part, change):
        for o in halves:

            @pl.when(zi == owners[o])
            def _():
                for z in others(o):
                    owned_from(turn, part, o, z).wait_recv()
                total = None
                for z in range(n_cand):
                    own = z == owners[o]
                    value = rs_send[turn, part, o] if own else rs_slots[turn, part, z]
                    total = value if total is None else total + value
                ag_slots[turn, part, o] = change(mass[of(part), half(o)] / total)
                for z in others(o):
                    from_owner(turn, part, o, z).start()

    def gathered(turn, part, o):
        @pl.when(zi != owners[0] + o)
        def _():
            from_owner(turn, part, o, owners[0] + o).wait_recv()

    def drain(turn, part):
        for o in halves:

            @pl.when(zi != owners[o])
            def _():
                to_owner(turn, part, o).wait_send()

            @pl.when(zi == owners[o])
            def _():
                for z in others(o):
                    from_owner(turn, part, o, z).wait_send()

    def cand_send(turn, part):
        total = None
        for o in (near, far):
            gathered(turn, part, o)
            value = contract_last(split_rows(ag_slots[turn, part, o]), k_two[:, half(o)])
            total = value if total is None else total + value
        cand_slots[turn, part, 0] = join_rows(total)
        return x_start(cand_slots.at[turn, part], 2 + turn * parts + part)

    def cand_finish(copies, turn, part):
        arrive(copies)
        cand_sums[of(part), :] = x_sum(cand_slots.at[turn, part])

    def keep(scale):
        return scale

    each = range(parts)
    for part in each:
        tgt_send(k_one, 0, part)
    changes = (jnp.square,) + (keep,) * (ITERS - 1)
    for turn in range(ITERS):
        for part in each:
            tgt_finish(turn, part, changes[turn])
        summed = [cand_send(turn, part) for part in each]
        for part in each:
            cand_finish(summed[part], turn, part)
            tgt_send(k_two, 1 + turn, part)
    out_cand[...] = -jnp.log(cand_sums[...])
    for part in each:
        tgt_finish(ITERS, part, jnp.log)
    for part in each:
        for o in halves:
            gathered(ITERS, part, o)
            out_tgt[of(part), half(o)] = ag_slots[ITERS, part, o]
    for turn in range(1 + ITERS):
        for part in each:
            drain(turn, part)
    for copy in pending + row_copies:
        copy.wait_send()


def fused(candidates, targets, member, mix_weight):
    n_tgt, n_cand = lax.axis_size("tgt"), lax.axis_size("cand")
    rows, width = candidates.shape
    cols = targets.shape[0]
    mixes, tasks = mix_weight.shape
    n_mix = lax.axis_size("mix")
    share = cols // 2
    parts = 2 if mixes % 16 == 0 else 1
    group = mixes // parts
    return tuple(pl.pallas_call(
        functools.partial(fused_kernel, n_tgt, n_cand, n_mix, parts),
        out_shape=(
            jax.ShapeDtypeStruct((mixes, rows), F32),
            jax.ShapeDtypeStruct((mixes, cols), F32),
        ),
        in_specs=[pl.BlockSpec(memory_space=pltpu.HBM)] * 2
        + [pl.BlockSpec(memory_space=pltpu.VMEM)] * 2,
        out_specs=(pl.BlockSpec(memory_space=pltpu.VMEM),) * 2,
        scratch_shapes=[
            pltpu.VMEM((rows, width), BF16),
            pltpu.VMEM((cols, width), BF16),
            pltpu.VMEM((cols, width), BF16),
            pltpu.VMEM((rows, cols), F32),
            pltpu.VMEM((rows, cols), BF16),
            pltpu.VMEM((rows, cols), BF16),
            pltpu.VMEM((mixes, cols), F32),
            pltpu.VMEM((mixes, rows), F32),
            pltpu.VMEM((n_mix, 1, rows // n_mix), F32),
            pltpu.VMEM((n_tgt, n_mix, 1, rows // n_mix), F32),
            pltpu.VMEM((n_cand, 1, cols), F32),
            pltpu.VMEM((n_tgt, tasks, rows), F32),
            pltpu.VMEM((ITERS, parts, n_tgt, group, rows), F32),
            pltpu.VMEM((1 + ITERS, parts, 2, group, share), F32),
            pltpu.VMEM((1 + ITERS, parts, n_cand, group, share), F32),
            pltpu.VMEM((1 + ITERS, parts, 2, group, share), F32),
            pltpu.SemaphoreType.DMA((2, max(rows, cols) // 256)),
            pltpu.SemaphoreType.DMA((2 + ITERS * parts, n_tgt - 1)),
            pltpu.SemaphoreType.DMA((2 + ITERS * parts, n_tgt - 1)),
            pltpu.SemaphoreType.DMA((1, n_cand - 1)),
            pltpu.SemaphoreType.DMA((1, n_cand - 1)),
            pltpu.SemaphoreType.DMA((n_tgt - 1, n_mix)),
            pltpu.SemaphoreType.DMA((n_tgt - 1, n_mix)),
            pltpu.SemaphoreType.DMA((1 + ITERS, parts, 2)),
            pltpu.SemaphoreType.DMA((1 + ITERS, parts, n_cand)),
            pltpu.SemaphoreType.DMA((1 + ITERS, parts, n_cand)),
            pltpu.SemaphoreType.DMA((1 + ITERS, parts, 2)),
        ],
        compiler_params=pltpu.CompilerParams(
            collective_id=0, has_side_effects=True, vmem_limit_bytes=56 * 1024 * 1024
        ),
    )(candidates, targets, member.reshape(1, -1), mix_weight.T))


def target_mass(own_member, member, mix_weight, cand_total):
    task_ids = jnp.arange(mix_weight.shape[1], dtype=jnp.int32)
    counts = jnp.sum((member[None, :] == task_ids[:, None]).astype(jnp.float32), axis=1)
    weight_total = jnp.dot(mix_weight, counts, precision=lax.Precision.HIGHEST)
    onehot = (own_member[None, :] == task_ids[:, None]).astype(jnp.float32)
    per_target = jnp.dot(mix_weight, onehot, precision=lax.Precision.HIGHEST)
    return per_target * (cand_total / weight_total)[:, None]


def by_collectives(candidates, targets, member, mix_weight):
    cand_rows = candidates.shape[0]
    tgt_rows = targets.shape[0]
    tgt_total = tgt_rows * lax.axis_size("tgt")
    cand_total = cand_rows * lax.axis_size("cand")
    tgt_unit = unit_rows(targets)
    scores = contract_last(unit_rows(candidates), tgt_unit)
    own_member = lax.dynamic_slice_in_dim(member, lax.axis_index("tgt") * tgt_rows, tgt_rows, 0)
    mass = target_mass(own_member, member, mix_weight, float(cand_total))
    kernel_one = jnp.exp(scores / EPS_FIRST) / tgt_total
    kernel_two = jnp.exp(scores / EPS_SECOND) / tgt_total
    scale_tgt = jnp.ones((mix_weight.shape[0], tgt_rows), jnp.float32)
    scale_cand = jnp.ones((mix_weight.shape[0], cand_rows), jnp.float32)
    for section_index, kernel in enumerate((kernel_one, kernel_two)):
        if section_index == 1:
            scale_tgt = scale_tgt * scale_tgt
        for repeat in range(ITERS):
            partial_value = lax.dot_general(
                scale_tgt, kernel, (((1,), (1,)), ((), ())), precision=lax.Precision.HIGHEST
            )
            scale_cand = 1.0 / lax.psum(partial_value, "tgt")
            column_part = jnp.dot(scale_cand, kernel, precision=lax.Precision.HIGHEST)
            share_cols = tgt_rows // lax.axis_size("cand")
            summed = lax.psum_scatter(column_part, "cand", scatter_dimension=1, tiled=True)
            own_mass = lax.dynamic_slice_in_dim(
                mass, lax.axis_index("cand") * share_cols, share_cols, 1
            )
            scale_tgt = lax.all_gather(own_mass / summed, "cand", axis=1, tiled=True)
    return (jnp.log(scale_cand), jnp.log(scale_tgt))


def solution(mesh):
    in_specs = (
        P(("groups", "cand"), None),
        P(("groups", "tgt"), None),
        P("groups"),
        P("mix", "groups"),
    )
    out_specs = (P("mix", ("groups", "cand")), P("mix", ("groups", "tgt")))
    n_tgt, n_cand = mesh.shape["tgt"], mesh.shape["cand"]

    def local(candidates, targets, member, mix_weight):
        lanes = targets.shape[0] % (128 * n_cand) == 0 and candidates.shape[0] % 512 == 0
        step = fused if lanes and n_cand % 2 == 0 and n_tgt > 1 else by_collectives
        return step(candidates, targets, member, mix_weight)

    return jax.shard_map(local, mesh=mesh, in_specs=in_specs, out_specs=out_specs, check_vma=False)
```
